32 devices in a mesh: groups: 2 (over x), tm: 16 (over z, y, core).
Axes of the slice: x: 2, y: 2, z: 4, core: 2. Of those that a mesh axis runs over, the one named last changes fastest.
Arguments:
- latent: bfloat16 [16384, 384], P(('groups', 'tm')), parts along dimension 0, may hold values from -45 to 45
- owner: int32 [16384], P(('groups', 'tm')), parts along dimension 0, may hold values from 0 to 15, as said below
- frame_counts: int32 [16], P('groups'), parts along dimension 0, may hold values from 1 to 8, 32 in all
- norm_gain: float32 [384], replicated, may hold values from 0.1 to 1.9
- norm_shift: float32 [384], replicated, may hold values from -3 to 3
- res_kernel: bfloat16 [3, 3, 3, 384, 384], replicated, may hold values from -0.0625 to 0.0625
- res_bias: float32 [384], replicated, may hold values from -3 to 3
- time_kernel: bfloat16 [3, 384, 768], replicated, may hold values from -0.1875 to 0.1875
- time_bias: float32 [768], replicated, may hold values from -3 to 3
- up_kernel: bfloat16 [3, 3, 384, 192], replicated, may hold values from -0.109375 to 0.109375
- up_bias: float32 [192], replicated, may hold values from -3 to 3
Outputs:
- frames_out: bfloat16 [128, 32, 6144], P(('groups', 'tm')), parts along dimension 0
The draws below stay inside these ranges and needn't reach their ends.
There are 2 independent parts, one for each index of `groups`. The reference program is written for one: setup_inputs(seed, part) draws one part's arguments, and reference() takes and returns one part's arrays. A program takes and returns all parts, laid end to end along the dimension named above; an argument that names none is the same for every part. Nothing has to cross between parts.
Inputs may be any that keep to these rules, and one draw needn't show every extreme that they name: Each device's block of 512 tokens holds at most 64 tokens for any one owner, some block holds exactly 64 for one owner, and every device is the owner of exactly 512 tokens.
All inputs are finite; a program needn't handle non-finite values.
Results may differ from the reference program's by a relative error of at most 0.0057.
Values may be sent and summed in bfloat16 or wider, within the bound.
A program may use at most 128 MiB of HBM per device.

```python
import math
import jax
import jax.numpy as jnp
import numpy as np
from jax import lax

C = 384
OC = 192
VIDEOS = 8
FR_DEV = 2
H = 16
W = 16
TC = 768
FRAMES = 32
N_TM = 16


def owner_table(key):
    peer_count = N_TM
    token_count = FR_DEV * H * W
    capacity = 2 * token_count // peer_count
    half_count = peer_count // 2
    first_key, second_key, third_key = jax.random.split(jax.random.fold_in(key, 11), 3)
    swings = jax.random.randint(first_key, (half_count,), -(capacity // 2), capacity // 2 + 1)
    summit = jax.random.randint(second_key, (), 0, half_count)
    swings = jnp.where(jnp.arange(half_count) == summit, capacity // 2, swings)
    distance = (jnp.arange(peer_count)[:, None] - jnp.arange(peer_count)[None, :]) % peer_count
    polarity = jnp.where(distance % 2 == 0, 1, -1)
    counts = capacity // 2 + polarity * swings[distance // 2]
    bounds = jnp.cumsum(counts, 1)
    orders = jax.vmap(lambda single: jax.random.permutation(single, token_count))(jax.random.split(third_key, peer_count))
    owners = jnp.sum((bounds[:, None, :] <= orders[:, :, None]).astype(jnp.int32), 2)
    return owners.reshape(-1).astype(jnp.int32)


def draw_owner(key, part):
    return owner_table(key)


def draw_latent(key, part):
    owners = owner_table(key)
    ranking = jnp.argsort(owners, stable=True)
    base_key, channel_key, pixel_key = jax.random.split(jax.random.fold_in(key, 23), 3)
    frame_count = FR_DEV * N_TM
    values = jax.random.truncated_normal(base_key, -3.0, 3.0, (frame_count, H * W, C), jnp.float32)
    pixel_scale = jnp.exp(jax.random.uniform(pixel_key, (frame_count, H * W, 1), jnp.float32, jnp.log(0.5), jnp.log(5.0)))
    channel_scale = jnp.exp(jax.random.uniform(channel_key, (C,), jnp.float32, jnp.log(0.5), jnp.log(5.0)))
    frame_scale = 3.0 ** (jnp.arange(frame_count, dtype=jnp.float32) / max(frame_count - 1, 1))
    values = 0.2 * values * channel_scale * pixel_scale * frame_scale[:, None, None]
    flattened = values.reshape(frame_count * H * W, C)
    return jnp.zeros_like(flattened).at[ranking].set(flattened).astype(jnp.bfloat16)


def split_up(amount, total, reach, slope):
    loads = [(1 << 20) // math.isqrt(standing ** slope) + 1 for standing in range(2, amount + 1)]
    rest, holding = total - reach - (amount - 1), [1] * (amount - 1)
    while rest > 0:
        free = [i for i in range(amount - 1) if holding[i] < reach]
        mass, budget = sum([loads[i] for i in free]), rest
        for i in free:
            extra = min(reach - holding[i], max(1, budget * loads[i] // mass), rest)
            holding[i] = holding[i] + extra
            rest = rest - extra
    return np.array([reach] + holding)


def uneven_parts(key, count, total, reach, lean):
    if count == 2:
        one = jax.random.randint(key, (), max(1, total - reach), min(reach, total - 1) + 1)
        return jnp.stack([one, total - one])
    tallies = jnp.asarray(split_up(count, total, reach, lean), jnp.int32)
    couples = (count - 1) // 2
    source_of, taker = tallies[1:1 + 2 * couples:2], tallies[2:2 + 2 * couples:2]
    room = jnp.minimum(source_of - 1, reach - taker)
    moved = jax.random.randint(jax.random.fold_in(key, 1), (couples,), 0, 1 << 20) % (room + 1)
    tallies = tallies.at[1:1 + 2 * couples:2].set(source_of - moved).at[2:2 + 2 * couples:2].set(taker + moved)
    return tallies[jax.random.permutation(jax.random.fold_in(key, 2), count)]


def noise(own_key, shape, spread, most, kind=jnp.bfloat16):
    return jnp.clip(spread * jax.random.normal(own_key, shape, jnp.float32), -most, most).astype(kind)


def setup_inputs(seed: int = 0, part: int = 0) -> dict:
    key_list = jax.random.split(jax.random.key(seed), 12)
    own_keys = jax.random.split(jax.random.fold_in(key_list[11], part), 12)
    latent = draw_latent(jax.random.fold_in(jax.random.fold_in(key_list[11], part), 71), part)
    owner = draw_owner(jax.random.fold_in(jax.random.fold_in(key_list[11], part), 71), part)
    frame_counts = uneven_parts(own_keys[2], VIDEOS, FRAMES, FRAMES // 4, 2).astype(jnp.int32)
    norm_gain = jnp.clip(1.0 + 0.18 * jax.random.normal(key_list[3], (C,), jnp.float32), 0.1, 1.9)
    norm_shift = noise(key_list[4], (C,), 0.5, 3.0, jnp.float32)
    res_kernel = noise(key_list[5], (3, 3, 3, C, C), (27 * C) ** -0.5, 0.0625)
    res_bias = noise(key_list[6], (C,), 0.5, 3.0, jnp.float32)
    time_kernel = noise(key_list[7], (3, C, TC), (3 * C) ** -0.5, 0.1875)
    time_bias = noise(key_list[8], (TC,), 0.5, 3.0, jnp.float32)
    up_kernel = noise(key_list[9], (3, 3, C, OC), (9 * C) ** -0.5, 0.109375)
    up_bias = noise(key_list[10], (OC,), 0.5, 3.0, jnp.float32)
    return {"latent": latent, "owner": owner, "frame_counts": frame_counts, "norm_gain": norm_gain, "norm_shift": norm_shift, "res_kernel": res_kernel, "res_bias": res_bias, "time_kernel": time_kernel, "time_bias": time_bias, "up_kernel": up_kernel, "up_bias": up_bias}


epsilon = 1e-06

def video_starts_of(frame_ids, frame_counts):
    video_ends = jnp.cumsum(frame_counts).astype(jnp.int32)
    video_starts = (video_ends - frame_counts).astype(jnp.int32)
    passed = lax.optimization_barrier(jnp.sum((video_ends[None, :] <= frame_ids[:, None]).astype(jnp.int32), 1)).astype(jnp.int32)
    member = jnp.minimum(passed, VIDEOS - 1)
    chosen = member[:, None] == jnp.arange(VIDEOS, dtype=jnp.int32)[None, :]
    return lax.optimization_barrier(jnp.sum(jnp.where(chosen, video_starts[None, :], 0), 1)).astype(jnp.int32)

def spatial_taps(frame_block, kernel):
    frames, height, columns, channels_in = frame_block.shape
    padded = jnp.pad(frame_block, ((0, 0), (1, 1), (1, 1), (0, 0)))
    summed = jnp.zeros((frames * height * columns, kernel.shape[-1]), jnp.float32)
    for row_tap in range(3):
        for col_tap in range(3):
            window = padded[:, row_tap:row_tap + height, col_tap:col_tap + columns, :]
            summed = summed + jnp.dot(window.reshape(-1, channels_in), kernel[row_tap, col_tap], preferred_element_type=jnp.float32)
    return summed

def causal_shift(field, starts, offset):
    frame_count = field.shape[0]
    moved = jnp.concatenate([jnp.zeros((offset,) + field.shape[1:], field.dtype), field[:frame_count - offset]], 0)
    keeping = (jnp.arange(frame_count, dtype=jnp.int32) - offset >= starts).astype(field.dtype)
    return moved * keeping.reshape((frame_count,) + (1,) * (field.ndim - 1))

def reference(latent, owner, frame_counts, norm_gain, norm_shift, res_kernel, res_bias, time_kernel, time_bias, up_kernel, up_bias):
    ranking = jnp.argsort(owner, stable=True)
    decoded = latent[ranking].reshape(FRAMES, H, W, C)
    starts = video_starts_of(jnp.arange(FRAMES, dtype=jnp.int32), frame_counts)
    values = decoded.astype(jnp.float32)
    squares = lax.optimization_barrier(jnp.mean(values * values, -1, keepdims=True))
    scaled = values * lax.rsqrt(squares + epsilon)
    activated = jax.nn.silu(scaled * norm_gain + norm_shift).astype(jnp.bfloat16)
    conv_sum = jnp.zeros((FRAMES * H * W, C), jnp.float32)
    for time_tap in range(3):
        conv_sum = conv_sum + spatial_taps(causal_shift(activated, starts, 2 - time_tap), res_kernel[time_tap])
    residual = (values.reshape(-1, C) + res_bias + conv_sum).astype(jnp.bfloat16).reshape(FRAMES, H, W, C)
    temporal = jnp.zeros((FRAMES * H * W, TC), jnp.float32)
    for time_tap in range(3):
        shifted = causal_shift(residual, starts, 2 - time_tap).reshape(-1, C)
        temporal = temporal + jnp.dot(shifted, time_kernel[time_tap], preferred_element_type=jnp.float32)
    temporal = (temporal + time_bias).astype(jnp.bfloat16)
    doubled = temporal.reshape(FRAMES, H, W, 2, C).transpose(0, 3, 1, 2, 4).reshape(2 * FRAMES, H, W, C)
    blocks = doubled.reshape(N_TM, 2 * FR_DEV, H, W, C)

    def upscale(frame_block):
        enlarged = jnp.repeat(jnp.repeat(frame_block, 2, axis=1), 2, axis=2)
        summed = spatial_taps(enlarged, up_kernel) + up_bias
        return summed.astype(jnp.bfloat16).reshape(2 * FR_DEV, 2 * H, 2 * W * OC)
    return lax.map(upscale, blocks).reshape(2 * FRAMES, 2 * H, 2 * W * OC)
```

```python
import functools
import math

import jax
import jax.numpy as jnp
from jax import lax
from jax.experimental import pallas as pl
from jax.experimental.pallas import tpu as pltpu
from jax.sharding import PartitionSpec as P

H = 16
W = 16
PIXELS = H * W
FRAMES_HERE = 2
MESH = pl.DeviceIdType.MESH

epsilon = 1e-06


def kernel(
    n,
    owner_ref,
    counts_ref,
    latent_ref,
    gain_ref,
    shift_ref,
    res_bias_ref,
    time_bias_ref,
    up_bias_ref,
    res_hbm,
    time_hbm,
    up_hbm,
    out_ref,
    res_w,
    time_w,
    up_raw,
    up_w,
    packed,
    recv,
    order,
    meta_out,
    meta_in,
    acc,
    pass_out,
    pass_in,
    resid_own,
    resid_halo,
    windows,
    temporal,
    enlarged,
    woven,
    stack_w,
    bias_row,
    load_sem,
    send_sem,
    recv_sem,
    meta_send_sem,
    meta_recv_sem,
    halo_send_sem,
    halo_recv_sem,
):
    me = lax.axis_index("tm")
    tokens, channels = latent_ref.shape
    chunks, _, capacity, cut = packed.shape
    slots = n * capacity
    up_channels = up_raw.shape[2]
    pair = 2 * up_channels
    f32, bf16 = jnp.float32, jnp.bfloat16

    barrier = pltpu.get_barrier_semaphore()

    @pl.loop(1, n)
    def _(k):
        pl.semaphore_signal(
            barrier, inc=1, device_id={"tm": lax.rem(me + k, n)}, device_id_type=MESH
        )

    loads = [
        pltpu.make_async_copy(src, dst, load_sem.at[i])
        for i, (src, dst) in enumerate(((up_hbm, up_raw), (res_hbm, res_w), (time_hbm, time_w)))
    ]
    for load in loads:
        load.start()

    owner = owner_ref[...]
    relative = lax.rem(owner - me + n, n)
    peers = lax.broadcasted_iota(jnp.int32, (n, tokens), 0)
    marked = (relative == peers).astype(f32)
    earlier = (
        lax.broadcasted_iota(jnp.int32, (tokens, tokens), 0)
        < lax.broadcasted_iota(jnp.int32, (tokens, tokens), 1)
    ).astype(f32).astype(bf16)
    before = jnp.dot(marked.astype(bf16), earlier, preferred_element_type=f32)
    rank = jnp.sum(before * marked, 0, keepdims=True).astype(jnp.int32)
    position = relative * capacity + rank

    per_group = 128 // capacity
    squares = latent_ref[...].astype(f32)
    squares = jnp.mean(squares * squares, -1, keepdims=True)
    scales = jnp.broadcast_to(lax.rsqrt(squares + epsilon), (tokens, 128)).T[0:1]
    lane = lax.rem(me, per_group) * capacity + rank
    lanes = lax.broadcasted_iota(jnp.int32, (128, tokens), 0)
    in_lane = (lanes == lane).astype(f32).astype(bf16)
    rest, scale_rows = scales, None
    for _ in range(3):
        piece = rest.astype(bf16).astype(f32)
        rest = rest - piece
        term = lax.dot_general(
            (marked * piece).astype(bf16),
            in_lane,
            (((1,), (1,)), ((), ())),
            preferred_element_type=f32,
        )
        scale_rows = term if scale_rows is None else scale_rows + term
    meta_out[...] = scale_rows[:, None, :]
    part = min(slots, 256)
    for c in range(slots // part):
        rows = lax.broadcasted_iota(jnp.int32, (part, tokens), 0) + c * part
        chosen = (rows == position).astype(f32).astype(bf16)
        block = jnp.dot(chosen, latent_ref[...], preferred_element_type=f32)
        per = part // capacity
        for i in range(chunks):
            packed[i, c * per : (c + 1) * per] = (
                block[:, i * cut : (i + 1) * cut].reshape(per, capacity, cut).astype(bf16)
            )

    pl.semaphore_wait(barrier, n - 1)

    @pl.loop(1, n)
    def _(k):
        peer = lax.rem(me + k, n)
        pltpu.make_async_remote_copy(
            src_ref=meta_out.at[k],
            dst_ref=meta_in.at[me],
            send_sem=meta_send_sem,
            recv_sem=meta_recv_sem,
            device_id={"tm": peer},
            device_id_type=MESH,
        ).start()

    for i in range(chunks):

        @pl.loop(1, n)
        def _(k):
            pltpu.make_async_remote_copy(
                src_ref=packed.at[i, k],
                dst_ref=recv.at[i, me],
                send_sem=send_sem.at[i],
                recv_sem=recv_sem.at[i],
                device_id={"tm": lax.rem(me + k, n)},
                device_id_type=MESH,
            ).start()

    meta_in[me] = meta_out[0]
    for i in range(chunks):
        recv[i, me] = packed[i, 0]

    border = jnp.zeros((H, 3 * cut), bf16)
    for i in range(chunks):
        for f in range(FRAMES_HERE):
            windows[i, f, 0:H] = border
            windows[i, f, H + PIXELS : 2 * H + PIXELS] = border

    @pl.when(me == 0)
    def _():
        pass_in[...] = jnp.zeros_like(pass_in)
        resid_halo[...] = jnp.zeros_like(resid_halo)

    bias_row[...] = jnp.zeros_like(bias_row)
    bias_row[0:1, 0:up_channels] = up_bias_ref[...][None, :]
    loads[0].wait()
    folds = (((0,), (1, 2)), ((0, 1), (2,)))
    columns = ((1, 2), (0, 1), (0,), (2,))
    for p in range(2):
        for i in range(2):
            for r, taps in enumerate(columns):
                total = None
                for a in folds[p][i]:
                    for b in taps:
                        term = up_raw[a, b].astype(f32)
                        total = term if total is None else total + term
                stack_w[r * up_channels : (r + 1) * up_channels] = total
            for t in range(2 * pair // 128):
                up_w[p, i * channels : (i + 1) * channels, t * 128 : (t + 1) * 128] = (
                    stack_w[t * 128 : (t + 1) * 128].T.astype(bf16)
                )

    first = me * FRAMES_HERE
    keep = []
    for f in range(2 * FRAMES_HERE):
        start = jnp.int32(0)
        begin = jnp.int32(0)
        for v in range(counts_ref.shape[0]):
            start = jnp.where(begin <= first + f, begin, start)
            begin = begin + counts_ref[v]
        keep.append(
            [jnp.where(first + f - 2 + j >= start, 1.0, 0.0).astype(f32) for j in range(2)]
        )

    def wait_all(src, dst, s_sem, r_sem):
        both = pltpu.make_async_remote_copy(
            src_ref=src.at[pl.ds(0, n - 1)],
            dst_ref=dst.at[pl.ds(0, n - 1)],
            send_sem=s_sem,
            recv_sem=r_sem,
            device_id={"tm": lax.rem(me + 1, n)},
            device_id_type=MESH,
        )
        both.wait_recv()
        both.wait_send()

    wait_all(meta_out, meta_in, meta_send_sem, meta_recv_sem)
    given = jnp.sum(jnp.where(meta_in[:, 0, :] > 0.0, 1.0, 0.0), 1, keepdims=True)
    slot = lax.broadcasted_iota(jnp.int32, (n, slots), 1)
    source = lax.broadcasted_iota(jnp.int32, (n, slots), 0)
    of_slot = slot // capacity
    here = jnp.sum(jnp.where(of_slot == source, given, 0.0), 0, keepdims=True).astype(jnp.int32)
    ahead = jnp.sum(jnp.where(source < of_slot, given, 0.0), 0, keepdims=True).astype(jnp.int32)
    row = lax.rem(slot[0:1], capacity)
    place = ahead + row
    pixel = lax.rem(place, PIXELS)
    place = place - pixel + lax.rem(pixel, W) * H + pixel // W
    place = jnp.where(row < here, place, -1)

    scale_of = jnp.concatenate(
        [
            jnp.sum(meta_in[g * per_group : (g + 1) * per_group, 0, :], 0, keepdims=True)
            for g in range(slots // 128)
        ],
        1,
    )
    row_scale = []
    for f in range(FRAMES_HERE):
        rows = lax.broadcasted_iota(jnp.int32, (PIXELS, slots), 0) + f * PIXELS
        chosen = rows == place
        order[f] = chosen.astype(f32).astype(bf16)
        row_scale.append(jnp.sum(jnp.where(chosen, scale_of, 0.0), 1, keepdims=True))
        acc[f] = jnp.broadcast_to(res_bias_ref[...][None, :], (PIXELS, channels))
        acc[FRAMES_HERE + f] = jnp.zeros((PIXELS, channels), f32)

    gain, shift = gain_ref[...][None, :], shift_ref[...][None, :]

    def store_shifted(target, top, value):
        width = value.shape[1]
        y_index = lax.rem(lax.broadcasted_iota(jnp.int32, value.shape, 0), H)
        above = jnp.where(y_index == 0, 0.0, pltpu.roll(value, 1, 0))
        below = jnp.where(y_index == H - 1, 0.0, pltpu.roll(value, PIXELS - 1, 0))
        for a, piece in enumerate((above, value, below)):
            target[top : top + PIXELS, a * width : (a + 1) * width] = piece.astype(bf16)

    right = lax.rem(me + 1, n)

    def hop(i, own, halo):
        return pltpu.make_async_remote_copy(
            src_ref=own,
            dst_ref=halo,
            send_sem=halo_send_sem.at[i],
            recv_sem=halo_recv_sem.at[i],
            device_id={"tm": right},
            device_id_type=MESH,
        )

    hops = (
        (0, pass_out.at[1], pass_in.at[1]),
        (1, pass_out.at[0], pass_in.at[0]),
        (2, resid_own.at[1], resid_halo.at[1]),
        (3, resid_own.at[0], resid_halo.at[0]),
    )

    def send(i):
        @pl.when(me < n - 1)
        def _():
            hop(*hops[i]).start()

    def receive(i):
        @pl.when(me > 0)
        def _():
            hop(*hops[i]).wait_recv()

    def sent(i):
        @pl.when(me < n - 1)
        def _():
            hop(*hops[i]).wait_send()

    def gathered(i):
        if capacity % 16:
            return recv[i].astype(f32).reshape(slots, cut).astype(bf16)
        return recv[i].reshape(slots, cut)

    def land(i, f, arrived):
        lo, hi = i * cut, (i + 1) * cut
        values = jnp.dot(order[f], arrived, preferred_element_type=f32)
        u = values * row_scale[f] * gain[:, lo:hi] + shift[:, lo:hi]
        act = (u / (1.0 + jnp.exp(-u))).astype(bf16)
        acc[f, :, lo:hi] += values
        store_shifted(windows.at[i, f], H, act.astype(f32))

    def taps(i, j, frames):
        lo, hi = i * cut, (i + 1) * cut
        weights = jnp.concatenate([res_w[j, a, b, lo:hi] for b in range(3) for a in range(3)], 0)
        lhs = jnp.concatenate(
            [
                windows[i, frames, b * H : b * H + PIXELS, :].reshape(-1, 3 * cut)
                for b in range(3)
            ],
            1,
        )
        return jnp.dot(lhs, weights, preferred_element_type=f32)

    both = slice(0, FRAMES_HERE)
    loads[1].wait()
    for i in range(chunks - 1):
        wait_all(packed.at[i], recv.at[i], send_sem.at[i], recv_sem.at[i])
        arrived = gathered(i)
        for f in range(FRAMES_HERE):
            land(i, f, arrived)
        acc[both] += taps(i, 2, both).reshape(FRAMES_HERE, PIXELS, channels)
        middle = taps(i, 1, both)
        acc[1] += keep[1][1] * middle[:PIXELS]
        acc[2] += keep[2][1] * middle[PIXELS:]
        last = taps(i, 0, both)
        acc[2] += keep[2][0] * last[:PIXELS]
        acc[3] += keep[3][0] * last[PIXELS:]

    i = chunks - 1
    wait_all(packed.at[i], recv.at[i], send_sem.at[i], recv_sem.at[i])
    arrived = gathered(i)
    early, late = slice(0, 1), slice(1, 2)
    land(i, 1, arrived)
    pass_out[1] = (acc[3] + keep[3][0] * taps(i, 0, late)).astype(bf16)
    send(0)
    land(i, 0, arrived)
    acc[2] += keep[2][1] * taps(i, 1, late)
    pass_out[0] = (acc[2] + keep[2][0] * taps(i, 0, early)).astype(bf16)
    send(1)
    acc[1] += taps(i, 2, late)
    acc[1] += keep[1][1] * taps(i, 1, early)
    acc[0] += taps(i, 2, early)

    loads[2].wait()
    time_bias = time_bias_ref[...][None, :]

    def mix(value, j):
        return jnp.dot(value, time_w[j], preferred_element_type=f32)

    receive(0)
    resid_own[1] = (acc[1] + pass_in[1].astype(f32)).astype(bf16)
    send(2)
    temporal[1] = mix(resid_own[1], 2) + time_bias
    receive(1)
    resid_own[0] = (acc[0] + pass_in[0].astype(f32)).astype(bf16)
    send(3)
    temporal[1] += keep[1][1] * mix(resid_own[0], 1)
    temporal[0] = mix(resid_own[0], 2) + time_bias

    bias = bias_row[...]
    bias = (bias + pltpu.roll(bias, up_channels, 1))[0:1]
    edge = jnp.zeros((H, 128), f32)
    lane_index = lax.broadcasted_iota(jnp.int32, (PIXELS, 128), 1)

    def enlarge(f):
        for half in range(2):
            frame = temporal[f, :, half * channels : (half + 1) * channels]
            store_shifted(enlarged.at[2 * f + half], 0, frame.astype(bf16).astype(f32))

    def upscale(f):
        for p in range(2):
            lhs = enlarged[2 * f : 2 * f + 2, :, p * channels : (p + 2) * channels]
            product = jnp.dot(
                lhs.reshape(2 * PIXELS, 2 * channels), up_w[p], preferred_element_type=f32
            )
            for half in range(2):
                rows = slice(half * PIXELS, (half + 1) * PIXELS)
                for t in range(pair // 128):
                    same = product[rows, t * 128 : (t + 1) * 128]
                    side = product[rows, pair + t * 128 : pair + (t + 1) * 128]
                    before_it = jnp.concatenate([edge, side[: PIXELS - H]], 0)
                    after_it = jnp.concatenate([side[H:], edge], 0)
                    if (t + 1) * 128 <= up_channels:
                        moved = before_it
                    elif t * 128 >= up_channels:
                        moved = after_it
                    else:
                        moved = jnp.where(lane_index < up_channels - t * 128, before_it, after_it)
                    woven[half, t, pl.ds(p, PIXELS, stride=2), :] = (
                        same + moved + bias[:, t * 128 : (t + 1) * 128]
                    )
        for half in range(2):
            for t in range(pair // 128):
                value = woven[half, t].astype(bf16)
                for x in range(W):
                    base = x * pair + t * 128
                    out_ref[2 * f + half, :, base : base + 128] = value[
                        x * 2 * H : (x + 1) * 2 * H
                    ]

    receive(2)
    temporal[1] += keep[1][0] * mix(resid_halo[1], 0)
    enlarge(1)
    upscale(1)
    temporal[0] += keep[0][1] * mix(resid_halo[1], 1)
    receive(3)
    temporal[0] += keep[0][0] * mix(resid_halo[0], 0)
    enlarge(0)
    upscale(0)

    for i in range(len(hops)):
        sent(i)


def on_device(
    latent,
    owner,
    frame_counts,
    norm_gain,
    norm_shift,
    res_kernel,
    res_bias,
    time_kernel,
    time_bias,
    up_kernel,
    up_bias,
):
    n = lax.axis_size("tm")
    tokens, channels = latent.shape
    capacity = 2 * tokens // n
    up_channels = up_kernel.shape[-1]
    cut = 128
    chunks = channels // cut
    f32, bf16 = jnp.float32, jnp.bfloat16
    vmem = pl.BlockSpec(memory_space=pltpu.VMEM)
    smem = pl.BlockSpec(memory_space=pltpu.SMEM)
    hbm = pl.BlockSpec(memory_space=pl.ANY)
    frame = (FRAMES_HERE, PIXELS)
    return pl.pallas_call(
        functools.partial(kernel, n),
        out_shape=pltpu.VMEM((2 * FRAMES_HERE, 2 * H, 2 * W * up_channels), bf16),
        in_specs=[vmem, smem, vmem, vmem, vmem, vmem, vmem, vmem, hbm, hbm, hbm],
        out_specs=vmem,
        scratch_shapes=[
            pltpu.VMEM(res_kernel.shape, bf16),
            pltpu.VMEM(time_kernel.shape, bf16),
            pltpu.VMEM((3, 3, up_channels, channels), bf16),
            pltpu.VMEM((2, 2 * channels, 4 * up_channels), bf16),
            pltpu.VMEM((chunks, n, capacity, cut), bf16),
            pltpu.VMEM((chunks, n, capacity, cut), bf16),
            pltpu.VMEM((*frame, n * capacity), bf16),
            pltpu.VMEM((n, 1, 128), f32),
            pltpu.VMEM((n, 1, 128), f32),
            pltpu.VMEM((2 * FRAMES_HERE, PIXELS, channels), f32),
            pltpu.VMEM((*frame, channels), bf16),
            pltpu.VMEM((*frame, channels), bf16),
            pltpu.VMEM((*frame, channels), bf16),
            pltpu.VMEM((*frame, channels), bf16),
            pltpu.VMEM((chunks, FRAMES_HERE, PIXELS + 2 * H, 3 * cut), bf16),
            pltpu.VMEM((*frame, 2 * channels), f32),
            pltpu.VMEM((2 * FRAMES_HERE, PIXELS, 3 * channels), bf16),
            pltpu.VMEM((2, 2 * up_channels // 128, 2 * PIXELS, 128), f32),
            pltpu.VMEM((4 * up_channels, channels), f32),
            pltpu.VMEM((8, 2 * up_channels), f32),
            pltpu.SemaphoreType.DMA((3,)),
            pltpu.SemaphoreType.DMA((chunks,)),
            pltpu.SemaphoreType.DMA((chunks,)),
            pltpu.SemaphoreType.DMA,
            pltpu.SemaphoreType.DMA,
            pltpu.SemaphoreType.DMA((4,)),
            pltpu.SemaphoreType.DMA((4,)),
        ],
        compiler_params=pltpu.CompilerParams(
            collective_id=0, has_side_effects=True, vmem_limit_bytes=60 << 20
        ),
    )(
        owner.reshape(1, tokens),
        frame_counts,
        latent,
        norm_gain,
        norm_shift,
        res_bias,
        time_bias,
        up_bias,
        res_kernel,
        time_kernel,
        up_kernel.swapaxes(2, 3),
    )


def solution(mesh):
    placed = (
        P(("groups", "tm"), None),
        P(("groups", "tm")),
        P("groups"),
        P(),
        P(),
        P(),
        P(),
        P(),
        P(),
        P(),
        P(),
    )
    return jax.shard_map(
        on_device,
        mesh=mesh,
        in_specs=placed,
        out_specs=P(("groups", "tm"), None, None),
        check_vma=False,
    )
```

```python
import functools
import math

import jax
import jax.numpy as jnp
from jax import lax
from jax.experimental import pallas as pl
from jax.experimental.pallas import tpu as pltpu
from jax.sharding import PartitionSpec as P

H = 16
W = 16
PIXELS = H * W
FRAMES_HERE = 2
MESH = pl.DeviceIdType.MESH

epsilon = 1e-06


def kernel(
    n,
    owner_ref,
    counts_ref,
    latent_ref,
    gain_ref,
    shift_ref,
    res_bias_ref,
    time_bias_ref,
    up_bias_ref,
    res_hbm,
    time_hbm,
    up_hbm,
    out_ref,
    res_w,
    time_w,
    up_raw,
    up_w,
    packed,
    recv,
    order,
    meta_out,
    meta_in,
    acc,
    act_own,
    act_halo,
    resid_own,
    resid_halo,
    windows,
    halo_windows,
    temporal,
    enlarged,
    woven,
    stack_w,
    bias_row,
    load_sem,
    send_sem,
    recv_sem,
    meta_send_sem,
    meta_recv_sem,
    halo_send_sem,
    halo_recv_sem,
):
    me = lax.axis_index("tm")
    tokens, channels = latent_ref.shape
    chunks, _, capacity, cut = packed.shape
    slots = n * capacity
    up_channels = up_raw.shape[2]
    pair = 2 * up_channels
    f32, bf16 = jnp.float32, jnp.bfloat16

    barrier = pltpu.get_barrier_semaphore()

    @pl.loop(1, n)
    def _(k):
        pl.semaphore_signal(
            barrier, inc=1, device_id={"tm": lax.rem(me + k, n)}, device_id_type=MESH
        )

    loads = [
        pltpu.make_async_copy(src, dst, load_sem.at[i])
        for i, (src, dst) in enumerate(((up_hbm, up_raw), (res_hbm, res_w), (time_hbm, time_w)))
    ]
    for load in loads:
        load.start()

    owner = owner_ref[...]
    relative = lax.rem(owner - me + n, n)
    peers = lax.broadcasted_iota(jnp.int32, (n, tokens), 0)
    marked = (relative == peers).astype(f32)
    earlier = (
        lax.broadcasted_iota(jnp.int32, (tokens, tokens), 0)
        < lax.broadcasted_iota(jnp.int32, (tokens, tokens), 1)
    ).astype(f32).astype(bf16)
    before = jnp.dot(marked.astype(bf16), earlier, preferred_element_type=f32)
    rank = jnp.sum(before * marked, 0, keepdims=True).astype(jnp.int32)
    position = relative * capacity + rank

    per_group = 128 // capacity
    squares = latent_ref[...].astype(f32)
    squares = jnp.mean(squares * squares, -1, keepdims=True)
    scales = jnp.broadcast_to(lax.rsqrt(squares + epsilon), (tokens, 128)).T[0:1]
    lane = lax.rem(me, per_group) * capacity + rank
    lanes = lax.broadcasted_iota(jnp.int32, (128, tokens), 0)
    in_lane = (lanes == lane).astype(f32).astype(bf16)
    rest, scale_rows = scales, None
    for _ in range(3):
        piece = rest.astype(bf16).astype(f32)
        rest = rest - piece
        term = lax.dot_general(
            (marked * piece).astype(bf16),
            in_lane,
            (((1,), (1,)), ((), ())),
            preferred_element_type=f32,
        )
        scale_rows = term if scale_rows is None else scale_rows + term
    meta_out[...] = scale_rows[:, None, :]
    part = min(slots, 256)
    for c in range(slots // part):
        rows = lax.broadcasted_iota(jnp.int32, (part, tokens), 0) + c * part
        chosen = (rows == position).astype(f32).astype(bf16)
        block = jnp.dot(chosen, latent_ref[...], preferred_element_type=f32)
        per = part // capacity
        for i in range(chunks):
            packed[i, c * per : (c + 1) * per] = (
                block[:, i * cut : (i + 1) * cut].reshape(per, capacity, cut).astype(bf16)
            )

    pl.semaphore_wait(barrier, n - 1)

    @pl.loop(1, n)
    def _(k):
        peer = lax.rem(me + k, n)
        pltpu.make_async_remote_copy(
            src_ref=meta_out.at[k],
            dst_ref=meta_in.at[me],
            send_sem=meta_send_sem,
            recv_sem=meta_recv_sem,
            device_id={"tm": peer},
            device_id_type=MESH,
        ).start()

    for i in range(chunks):

        @pl.loop(1, n)
        def _(k):
            pltpu.make_async_remote_copy(
                src_ref=packed.at[i, k],
                dst_ref=recv.at[i, me],
                send_sem=send_sem.at[i],
                recv_sem=recv_sem.at[i],
                device_id={"tm": lax.rem(me + k, n)},
                device_id_type=MESH,
            ).start()

    meta_in[me] = meta_out[0]
    for i in range(chunks):
        recv[i, me] = packed[i, 0]

    border = jnp.zeros((H, 3 * cut), bf16)
    for i in range(chunks):
        for f in range(FRAMES_HERE):
            windows[i, f, 0:H] = border
            windows[i, f, H + PIXELS : 2 * H + PIXELS] = border
            halo_windows[i, f, 0:H] = border
            halo_windows[i, f, H + PIXELS : 2 * H + PIXELS] = border

    @pl.when(me == 0)
    def _():
        act_halo[...] = jnp.zeros_like(act_halo)
        resid_halo[...] = jnp.zeros_like(resid_halo)

    bias_row[...] = jnp.zeros_like(bias_row)
    bias_row[0:1, 0:up_channels] = up_bias_ref[...][None, :]
    loads[0].wait()
    folds = (((0,), (1, 2)), ((0, 1), (2,)))
    columns = ((1, 2), (0, 1), (0,), (2,))
    for p in range(2):
        for i in range(2):
            for r, taps in enumerate(columns):
                total = None
                for a in folds[p][i]:
                    for b in taps:
                        term = up_raw[a, b].astype(f32)
                        total = term if total is None else total + term
                stack_w[r * up_channels : (r + 1) * up_channels] = total
            for t in range(2 * pair // 128):
                up_w[p, i * channels : (i + 1) * channels, t * 128 : (t + 1) * 128] = (
                    stack_w[t * 128 : (t + 1) * 128].T.astype(bf16)
                )

    first = me * FRAMES_HERE
    keep = []
    for f in range(FRAMES_HERE):
        start = jnp.int32(0)
        begin = jnp.int32(0)
        for v in range(counts_ref.shape[0]):
            start = jnp.where(begin <= first + f, begin, start)
            begin = begin + counts_ref[v]
        keep.append(
            [jnp.where(first + f - 2 + j >= start, 1.0, 0.0).astype(f32) for j in range(2)]
        )

    def wait_all(src, dst, s_sem, r_sem):
        both = pltpu.make_async_remote_copy(
            src_ref=src.at[pl.ds(0, n - 1)],
            dst_ref=dst.at[pl.ds(0, n - 1)],
            send_sem=s_sem,
            recv_sem=r_sem,
            device_id={"tm": lax.rem(me + 1, n)},
            device_id_type=MESH,
        )
        both.wait_recv()
        both.wait_send()

    wait_all(meta_out, meta_in, meta_send_sem, meta_recv_sem)
    given = jnp.sum(jnp.where(meta_in[:, 0, :] > 0.0, 1.0, 0.0), 1, keepdims=True)
    slot = lax.broadcasted_iota(jnp.int32, (n, slots), 1)
    source = lax.broadcasted_iota(jnp.int32, (n, slots), 0)
    of_slot = slot // capacity
    here = jnp.sum(jnp.where(of_slot == source, given, 0.0), 0, keepdims=True).astype(jnp.int32)
    ahead = jnp.sum(jnp.where(source < of_slot, given, 0.0), 0, keepdims=True).astype(jnp.int32)
    row = lax.rem(slot[0:1], capacity)
    place = ahead + row
    pixel = lax.rem(place, PIXELS)
    place = place - pixel + lax.rem(pixel, W) * H + pixel // W
    place = jnp.where(row < here, place, -1)

    scale_of = jnp.concatenate(
        [
            jnp.sum(meta_in[g * per_group : (g + 1) * per_group, 0, :], 0, keepdims=True)
            for g in range(slots // 128)
        ],
        1,
    )
    row_scale = []
    for f in range(FRAMES_HERE):
        rows = lax.broadcasted_iota(jnp.int32, (PIXELS, slots), 0) + f * PIXELS
        chosen = rows == place
        order[f] = chosen.astype(f32).astype(bf16)
        row_scale.append(jnp.sum(jnp.where(chosen, scale_of, 0.0), 1, keepdims=True))
        acc[f] = jnp.broadcast_to(res_bias_ref[...][None, :], (PIXELS, channels))

    gain, shift = gain_ref[...][None, :], shift_ref[...][None, :]

    def store_shifted(target, top, value):
        width = value.shape[1]
        y_index = lax.rem(lax.broadcasted_iota(jnp.int32, value.shape, 0), H)
        above = jnp.where(y_index == 0, 0.0, pltpu.roll(value, 1, 0))
        below = jnp.where(y_index == H - 1, 0.0, pltpu.roll(value, PIXELS - 1, 0))
        for a, piece in enumerate((above, value, below)):
            target[top : top + PIXELS, a * width : (a + 1) * width] = piece.astype(bf16)

    right = lax.rem(me + 1, n)

    def hop(i, own, halo):
        return pltpu.make_async_remote_copy(
            src_ref=own,
            dst_ref=halo,
            send_sem=halo_send_sem.at[i],
            recv_sem=halo_recv_sem.at[i],
            device_id={"tm": right},
            device_id_type=MESH,
        )

    hops = [(act_own.at[i], act_halo.at[i]) for i in range(chunks - 1)]
    for owned, halo in ((act_own.at[chunks - 1], act_halo.at[chunks - 1]), (resid_own, resid_halo)):
        hops += [(owned.at[1], halo.at[1]), (owned.at[0], halo.at[0])]
    last = chunks - 1
    resid = chunks + 1

    def send(i):
        @pl.when(me < n - 1)
        def _():
            hop(i, *hops[i]).start()

    def receive(i):
        @pl.when(me > 0)
        def _():
            hop(i, *hops[i]).wait_recv()

    def sent(i):
        @pl.when(me < n - 1)
        def _():
            hop(i, *hops[i]).wait_send()

    def gathered(i):
        if capacity % 16:
            return recv[i].astype(f32).reshape(slots, cut).astype(bf16)
        return recv[i].reshape(slots, cut)

    def land(i, f, arrived):
        lo, hi = i * cut, (i + 1) * cut
        values = jnp.dot(order[f], arrived, preferred_element_type=f32)
        u = values * row_scale[f] * gain[:, lo:hi] + shift[:, lo:hi]
        act = (u / (1.0 + jnp.exp(-u))).astype(bf16)
        acc[f, :, lo:hi] += values
        act_own[i, f] = act
        return act.astype(f32)

    def spread(i, f, act):
        store_shifted(windows.at[i, f], H, act)

    def taps(i, j, frames, source=windows):
        lo, hi = i * cut, (i + 1) * cut
        weights = jnp.concatenate([res_w[j, a, b, lo:hi] for b in range(3) for a in range(3)], 0)
        lhs = jnp.concatenate(
            [
                source[i, frames, b * H : b * H + PIXELS, :].reshape(-1, 3 * cut)
                for b in range(3)
            ],
            1,
        )
        return jnp.dot(lhs, weights, preferred_element_type=f32)

    both, early, late = slice(0, FRAMES_HERE), slice(0, 1), slice(1, 2)

    def own_taps(i):
        acc[...] += taps(i, 2, both).reshape(FRAMES_HERE, PIXELS, channels)
        acc[1] += keep[1][1] * taps(i, 1, early)

    def halo_taps():
        for i in range(chunks - 1):
            receive(i)
            for f in range(FRAMES_HERE):
                store_shifted(halo_windows.at[i, f], H, act_halo[i, f].astype(f32))
            oldest = taps(i, 0, both, halo_windows)
            acc[0] += keep[0][0] * oldest[:PIXELS]
            acc[1] += keep[1][0] * oldest[PIXELS:]
            acc[0] += keep[0][1] * taps(i, 1, late, halo_windows)

    paired = lax.rem(me, 2) == 1
    loads[1].wait()
    for i in range(chunks - 1):
        wait_all(packed.at[i], recv.at[i], send_sem.at[i], recv_sem.at[i])
        arrived = gathered(i)
        acts = [land(i, f, arrived) for f in range(FRAMES_HERE)]
        send(i)
        for f in range(FRAMES_HERE):
            spread(i, f, acts[f])
        own_taps(i)

    @pl.when(paired)
    def _():
        halo_taps()

    wait_all(packed.at[last], recv.at[last], send_sem.at[last], recv_sem.at[last])
    arrived = gathered(last)
    acts = {}
    for f in (1, 0):
        acts[f] = land(last, f, arrived)
        send(last + 1 - f)
    for f in (1, 0):
        spread(last, f, acts[f])
    own_taps(last)

    @pl.when(jnp.logical_not(paired))
    def _():
        halo_taps()

    loads[2].wait()
    time_bias = time_bias_ref[...][None, :]

    def mix(value, j):
        return jnp.dot(value, time_w[j], preferred_element_type=f32)

    receive(last)
    store_shifted(halo_windows.at[last, 1], H, act_halo[last, 1].astype(f32))
    resid_own[1] = (acc[1] + keep[1][0] * taps(last, 0, late, halo_windows)).astype(bf16)
    send(resid)
    acc[0] += keep[0][1] * taps(last, 1, late, halo_windows)
    receive(last + 1)
    store_shifted(halo_windows.at[last, 0], H, act_halo[last, 0].astype(f32))
    resid_own[0] = (acc[0] + keep[0][0] * taps(last, 0, early, halo_windows)).astype(bf16)
    send(resid + 1)
    temporal[1] = mix(resid_own[1], 2) + time_bias
    temporal[1] += keep[1][1] * mix(resid_own[0], 1)
    temporal[0] = mix(resid_own[0], 2) + time_bias

    bias = bias_row[...]
    bias = (bias + pltpu.roll(bias, up_channels, 1))[0:1]
    edge = jnp.zeros((H, 128), f32)
    lane_index = lax.broadcasted_iota(jnp.int32, (PIXELS, 128), 1)

    def enlarge(f):
        for half in range(2):
            frame = temporal[f, :, half * channels : (half + 1) * channels]
            store_shifted(enlarged.at[2 * f + half], 0, frame.astype(bf16).astype(f32))

    def upscale(f):
        for p in range(2):
            lhs = enlarged[2 * f : 2 * f + 2, :, p * channels : (p + 2) * channels]
            product = jnp.dot(
                lhs.reshape(2 * PIXELS, 2 * channels), up_w[p], preferred_element_type=f32
            )
            for half in range(2):
                rows = slice(half * PIXELS, (half + 1) * PIXELS)
                for t in range(pair // 128):
                    same = product[rows, t * 128 : (t + 1) * 128]
                    side = product[rows, pair + t * 128 : pair + (t + 1) * 128]
                    before_it = jnp.concatenate([edge, side[: PIXELS - H]], 0)
                    after_it = jnp.concatenate([side[H:], edge], 0)
                    if (t + 1) * 128 <= up_channels:
                        moved = before_it
                    elif t * 128 >= up_channels:
                        moved = after_it
                    else:
                        moved = jnp.where(lane_index < up_channels - t * 128, before_it, after_it)
                    woven[half, t, pl.ds(p, PIXELS, stride=2), :] = (
                        same + moved + bias[:, t * 128 : (t + 1) * 128]
                    )
        for half in range(2):
            for t in range(pair // 128):
                value = woven[half, t].astype(bf16)
                for x in range(W):
                    base = x * pair + t * 128
                    out_ref[2 * f + half, :, base : base + 128] = value[
                        x * 2 * H : (x + 1) * 2 * H
                    ]

    receive(resid)
    temporal[1] += keep[1][0] * mix(resid_halo[1], 0)
    enlarge(1)
    upscale(1)
    temporal[0] += keep[0][1] * mix(resid_halo[1], 1)
    receive(resid + 1)
    temporal[0] += keep[0][0] * mix(resid_halo[0], 0)
    enlarge(0)
    upscale(0)

    for i in range(len(hops)):
        sent(i)


def on_device(
    latent,
    owner,
    frame_counts,
    norm_gain,
    norm_shift,
    res_kernel,
    res_bias,
    time_kernel,
    time_bias,
    up_kernel,
    up_bias,
):
    n = lax.axis_size("tm")
    tokens, channels = latent.shape
    capacity = 2 * tokens // n
    up_channels = up_kernel.shape[-1]
    cut = 128
    chunks = channels // cut
    f32, bf16 = jnp.float32, jnp.bfloat16
    vmem = pl.BlockSpec(memory_space=pltpu.VMEM)
    smem = pl.BlockSpec(memory_space=pltpu.SMEM)
    hbm = pl.BlockSpec(memory_space=pl.ANY)
    frame = (FRAMES_HERE, PIXELS)
    return pl.pallas_call(
        functools.partial(kernel, n),
        out_shape=pltpu.VMEM((2 * FRAMES_HERE, 2 * H, 2 * W * up_channels), bf16),
        in_specs=[vmem, smem, vmem, vmem, vmem, vmem, vmem, vmem, hbm, hbm, hbm],
        out_specs=vmem,
        scratch_shapes=[
            pltpu.VMEM(res_kernel.shape, bf16),
            pltpu.VMEM(time_kernel.shape, bf16),
            pltpu.VMEM((3, 3, up_channels, channels), bf16),
            pltpu.VMEM((2, 2 * channels, 4 * up_channels), bf16),
            pltpu.VMEM((chunks, n, capacity, cut), bf16),
            pltpu.VMEM((chunks, n, capacity, cut), bf16),
            pltpu.VMEM((*frame, n * capacity), bf16),
            pltpu.VMEM((n, 1, 128), f32),
            pltpu.VMEM((n, 1, 128), f32),
            pltpu.VMEM((*frame, channels), f32),
            pltpu.VMEM((chunks, *frame, cut), bf16),
            pltpu.VMEM((chunks, *frame, cut), bf16),
            pltpu.VMEM((*frame, channels), bf16),
            pltpu.VMEM((*frame, channels), bf16),
            pltpu.VMEM((chunks, FRAMES_HERE, PIXELS + 2 * H, 3 * cut), bf16),
            pltpu.VMEM((chunks, FRAMES_HERE, PIXELS + 2 * H, 3 * cut), bf16),
            pltpu.VMEM((*frame, 2 * channels), f32),
            pltpu.VMEM((2 * FRAMES_HERE, PIXELS, 3 * channels), bf16),
            pltpu.VMEM((2, 2 * up_channels // 128, 2 * PIXELS, 128), f32),
            pltpu.VMEM((4 * up_channels, channels), f32),
            pltpu.VMEM((8, 2 * up_channels), f32),
            pltpu.SemaphoreType.DMA((3,)),
            pltpu.SemaphoreType.DMA((chunks,)),
            pltpu.SemaphoreType.DMA((chunks,)),
            pltpu.SemaphoreType.DMA,
            pltpu.SemaphoreType.DMA,
            pltpu.SemaphoreType.DMA((chunks + 3,)),
            pltpu.SemaphoreType.DMA((chunks + 3,)),
        ],
        compiler_params=pltpu.CompilerParams(
            collective_id=0, has_side_effects=True, vmem_limit_bytes=60 << 20
        ),
    )(
        owner.reshape(1, tokens),
        frame_counts,
        latent,
        norm_gain,
        norm_shift,
        res_bias,
        time_bias,
        up_bias,
        res_kernel,
        time_kernel,
        up_kernel.swapaxes(2, 3),
    )


def solution(mesh):
    placed = (
        P(("groups", "tm"), None),
        P(("groups", "tm")),
        P("groups"),
        P(),
        P(),
        P(),
        P(),
        P(),
        P(),
        P(),
        P(),
    )
    return jax.shard_map(
        on_device,
        mesh=mesh,
        in_specs=placed,
        out_specs=P(("groups", "tm"), None, None),
        check_vma=False,
    )
```

```python
import functools
import math

import jax
import jax.numpy as jnp
from jax import lax
from jax.experimental import pallas as pl
from jax.experimental.pallas import tpu as pltpu
from jax.sharding import PartitionSpec as P

H = 16
W = 16
PIXELS = H * W
FRAMES_HERE = 2
MESH = pl.DeviceIdType.MESH

epsilon = 1e-06


def kernel(
    n,
    owner_ref,
    counts_ref,
    latent_ref,
    gain_ref,
    shift_ref,
    res_bias_ref,
    time_bias_ref,
    up_bias_ref,
    res_hbm,
    time_hbm,
    up_hbm,
    out_ref,
    res_w,
    time_w,
    up_raw,
    up_w,
    packed,
    recv,
    order,
    meta_out,
    meta_in,
    acc,
    act_own,
    act_halo,
    resid_own,
    resid_halo,
    windows,
    halo_windows,
    temporal,
    enlarged,
    woven,
    stack_w,
    bias_row,
    load_sem,
    send_sem,
    recv_sem,
    meta_send_sem,
    meta_recv_sem,
    halo_send_sem,
    halo_recv_sem,
    known_sem,
):
    me = lax.axis_index("tm")
    tokens, channels = latent_ref.shape
    chunks, _, capacity, cut = packed.shape
    slots = n * capacity
    up_channels = up_raw.shape[2]
    pair = 2 * up_channels
    f32, bf16 = jnp.float32, jnp.bfloat16

    barrier = pltpu.get_barrier_semaphore()

    bits = [1 << b for b in range(n.bit_length() - 1)]
    assert n == 1 << len(bits)

    def partner(k):
        return me + sum(b * (1 - 2 * lax.rem(me // b, 2)) for b in bits if k & b)

    def greet(semaphore, k):
        pl.semaphore_signal(
            semaphore, inc=1, device_id={"tm": partner(k)}, device_id_type=MESH
        )

    for b in bits:
        greet(barrier, b)

    loads = [
        pltpu.make_async_copy(src, dst, load_sem.at[i])
        for i, (src, dst) in enumerate(((up_hbm, up_raw), (res_hbm, res_w), (time_hbm, time_w)))
    ]
    for load in loads:
        load.start()

    owner = owner_ref[...]
    relative = lax.rem(owner - me + n, n)
    peers = lax.broadcasted_iota(jnp.int32, (n, tokens), 0)
    marked = (relative == peers).astype(f32)
    earlier = (
        lax.broadcasted_iota(jnp.int32, (tokens, tokens), 0)
        < lax.broadcasted_iota(jnp.int32, (tokens, tokens), 1)
    ).astype(f32).astype(bf16)
    before = jnp.dot(marked.astype(bf16), earlier, preferred_element_type=f32)
    rank = jnp.sum(before * marked, 0, keepdims=True).astype(jnp.int32)
    position = relative * capacity + rank

    per_group = 128 // capacity
    squares = latent_ref[...].astype(f32)
    squares = jnp.mean(squares * squares, -1, keepdims=True)
    scales = jnp.broadcast_to(lax.rsqrt(squares + epsilon), (tokens, 128)).T[0:1]
    lane = lax.rem(me, per_group) * capacity + rank
    lanes = lax.broadcasted_iota(jnp.int32, (128, tokens), 0)
    in_lane = (lanes == lane).astype(f32).astype(bf16)
    rest, scale_rows = scales, None
    for _ in range(3):
        piece = rest.astype(bf16).astype(f32)
        rest = rest - piece
        term = lax.dot_general(
            (marked * piece).astype(bf16),
            in_lane,
            (((1,), (1,)), ((), ())),
            preferred_element_type=f32,
        )
        scale_rows = term if scale_rows is None else scale_rows + term
    meta_out[...] = scale_rows[:, None, :]
    part = min(slots, 256)
    for c in range(slots // part):
        rows = lax.broadcasted_iota(jnp.int32, (part, tokens), 0) + c * part
        chosen = (rows == position).astype(f32).astype(bf16)
        block = jnp.dot(chosen, latent_ref[...], preferred_element_type=f32)
        per = part // capacity
        for i in range(chunks):
            packed[i, c * per : (c + 1) * per] = (
                block[:, i * cut : (i + 1) * cut].reshape(per, capacity, cut).astype(bf16)
            )

    pl.semaphore_wait(barrier, len(bits))

    def post(i, peer):
        pltpu.make_async_remote_copy(
            src_ref=packed.at[i, lax.rem(peer - me + n, n)],
            dst_ref=recv.at[i, me],
            send_sem=send_sem.at[i],
            recv_sem=recv_sem.at[i],
            device_id={"tm": peer},
            device_id_type=MESH,
        ).start()

    def open_with(offsets):
        for k in sorted(offsets, reverse=True):
            peer = partner(k)
            pltpu.make_async_remote_copy(
                src_ref=meta_out.at[lax.rem(peer - me + n, n)],
                dst_ref=meta_in.at[me],
                send_sem=meta_send_sem,
                recv_sem=meta_recv_sem,
                device_id={"tm": peer},
                device_id_type=MESH,
            ).start()
            post(0, peer)

    known = set(bits)
    for r, b in enumerate(bits[:-1]):
        greet(known_sem.at[r], b)
        open_with(known if r == 0 else known - older)
        older = set(known)
        known |= {b ^ k for k in known if k != b}
        pl.semaphore_wait(known_sem.at[r], 1)
    open_with(known - older)

    for i in range(1, chunks):

        @pl.loop(1, n)
        def _(k):
            post(i, lax.rem(me + k, n))

    meta_in[me] = meta_out[0]
    for i in range(chunks):
        recv[i, me] = packed[i, 0]

    border = jnp.zeros((H, 3 * cut), bf16)
    for i in range(chunks):
        for f in range(FRAMES_HERE):
            windows[i, f, 0:H] = border
            windows[i, f, H + PIXELS : 2 * H + PIXELS] = border
            halo_windows[i, f, 0:H] = border
            halo_windows[i, f, H + PIXELS : 2 * H + PIXELS] = border

    @pl.when(me == 0)
    def _():
        act_halo[...] = jnp.zeros_like(act_halo)
        resid_halo[...] = jnp.zeros_like(resid_halo)

    bias_row[...] = jnp.zeros_like(bias_row)
    bias_row[0:1, 0:up_channels] = up_bias_ref[...][None, :]
    loads[0].wait()
    folds = (((0,), (1, 2)), ((0, 1), (2,)))
    columns = ((1, 2), (0, 1), (0,), (2,))
    for p in range(2):
        for i in range(2):
            for r, taps in enumerate(columns):
                total = None
                for a in folds[p][i]:
                    for b in taps:
                        term = up_raw[a, b].astype(f32)
                        total = term if total is None else total + term
                stack_w[r * up_channels : (r + 1) * up_channels] = total
            for t in range(2 * pair // 128):
                up_w[p, i * channels : (i + 1) * channels, t * 128 : (t + 1) * 128] = (
                    stack_w[t * 128 : (t + 1) * 128].T.astype(bf16)
                )

    first = me * FRAMES_HERE
    keep = []
    for f in range(FRAMES_HERE):
        start = jnp.int32(0)
        begin = jnp.int32(0)
        for v in range(counts_ref.shape[0]):
            start = jnp.where(begin <= first + f, begin, start)
            begin = begin + counts_ref[v]
        keep.append(
            [jnp.where(first + f - 2 + j >= start, 1.0, 0.0).astype(f32) for j in range(2)]
        )

    def wait_all(src, dst, s_sem, r_sem):
        both = pltpu.make_async_remote_copy(
            src_ref=src.at[pl.ds(0, n - 1)],
            dst_ref=dst.at[pl.ds(0, n - 1)],
            send_sem=s_sem,
            recv_sem=r_sem,
            device_id={"tm": lax.rem(me + 1, n)},
            device_id_type=MESH,
        )
        both.wait_recv()
        both.wait_send()

    wait_all(meta_out, meta_in, meta_send_sem, meta_recv_sem)
    given = jnp.sum(jnp.where(meta_in[:, 0, :] > 0.0, 1.0, 0.0), 1, keepdims=True)
    slot = lax.broadcasted_iota(jnp.int32, (n, slots), 1)
    source = lax.broadcasted_iota(jnp.int32, (n, slots), 0)
    of_slot = slot // capacity
    here = jnp.sum(jnp.where(of_slot == source, given, 0.0), 0, keepdims=True).astype(jnp.int32)
    ahead = jnp.sum(jnp.where(source < of_slot, given, 0.0), 0, keepdims=True).astype(jnp.int32)
    row = lax.rem(slot[0:1], capacity)
    place = ahead + row
    pixel = lax.rem(place, PIXELS)
    place = place - pixel + lax.rem(pixel, W) * H + pixel // W
    place = jnp.where(row < here, place, -1)

    scale_of = jnp.concatenate(
        [
            jnp.sum(meta_in[g * per_group : (g + 1) * per_group, 0, :], 0, keepdims=True)
            for g in range(slots // 128)
        ],
        1,
    )
    row_scale = []
    for f in range(FRAMES_HERE):
        rows = lax.broadcasted_iota(jnp.int32, (PIXELS, slots), 0) + f * PIXELS
        chosen = rows == place
        order[f] = chosen.astype(f32).astype(bf16)
        row_scale.append(jnp.sum(jnp.where(chosen, scale_of, 0.0), 1, keepdims=True))
        acc[f] = jnp.broadcast_to(res_bias_ref[...][None, :], (PIXELS, channels))

    gain, shift = gain_ref[...][None, :], shift_ref[...][None, :]

    def store_shifted(target, top, value):
        width = value.shape[1]
        y_index = lax.rem(lax.broadcasted_iota(jnp.int32, value.shape, 0), H)
        above = jnp.where(y_index == 0, 0.0, pltpu.roll(value, 1, 0))
        below = jnp.where(y_index == H - 1, 0.0, pltpu.roll(value, PIXELS - 1, 0))
        for a, piece in enumerate((above, value, below)):
            target[top : top + PIXELS, a * width : (a + 1) * width] = piece.astype(bf16)

    right = lax.rem(me + 1, n)

    def hop(i, own, halo):
        return pltpu.make_async_remote_copy(
            src_ref=own,
            dst_ref=halo,
            send_sem=halo_send_sem.at[i],
            recv_sem=halo_recv_sem.at[i],
            device_id={"tm": right},
            device_id_type=MESH,
        )

    hops = [(act_own.at[i], act_halo.at[i]) for i in range(chunks - 1)]
    for owned, halo in ((act_own.at[chunks - 1], act_halo.at[chunks - 1]), (resid_own, resid_halo)):
        hops += [(owned.at[1], halo.at[1]), (owned.at[0], halo.at[0])]
    last = chunks - 1
    resid = chunks + 1

    def send(i):
        @pl.when(me < n - 1)
        def _():
            hop(i, *hops[i]).start()

    def receive(i):
        @pl.when(me > 0)
        def _():
            hop(i, *hops[i]).wait_recv()

    def sent(i):
        @pl.when(me < n - 1)
        def _():
            hop(i, *hops[i]).wait_send()

    def gathered(i):
        if capacity % 16:
            return recv[i].astype(f32).reshape(slots, cut).astype(bf16)
        return recv[i].reshape(slots, cut)

    def land(i, f, arrived):
        lo, hi = i * cut, (i + 1) * cut
        values = jnp.dot(order[f], arrived, preferred_element_type=f32)
        u = values * row_scale[f] * gain[:, lo:hi] + shift[:, lo:hi]
        act = (u / (1.0 + jnp.exp(-u))).astype(bf16)
        acc[f, :, lo:hi] += values
        act_own[i, f] = act
        return act.astype(f32)

    def spread(i, f, act):
        store_shifted(windows.at[i, f], H, act)

    def taps(i, j, frames, source=windows):
        lo, hi = i * cut, (i + 1) * cut
        weights = jnp.concatenate([res_w[j, a, b, lo:hi] for b in range(3) for a in range(3)], 0)
        lhs = jnp.concatenate(
            [
                source[i, frames, b * H : b * H + PIXELS, :].reshape(-1, 3 * cut)
                for b in range(3)
            ],
            1,
        )
        return jnp.dot(lhs, weights, preferred_element_type=f32)

    both, early, late = slice(0, FRAMES_HERE), slice(0, 1), slice(1, 2)

    def own_taps(i):
        acc[...] += taps(i, 2, both).reshape(FRAMES_HERE, PIXELS, channels)
        acc[1] += keep[1][1] * taps(i, 1, early)

    def halo_taps():
        for i in range(chunks - 1):
            receive(i)
            for f in range(FRAMES_HERE):
                store_shifted(halo_windows.at[i, f], H, act_halo[i, f].astype(f32))
            oldest = taps(i, 0, both, halo_windows)
            acc[0] += keep[0][0] * oldest[:PIXELS]
            acc[1] += keep[1][0] * oldest[PIXELS:]
            acc[0] += keep[0][1] * taps(i, 1, late, halo_windows)

    paired = lax.rem(me, 2) == 1
    loads[1].wait()
    for i in range(chunks - 1):
        wait_all(packed.at[i], recv.at[i], send_sem.at[i], recv_sem.at[i])
        arrived = gathered(i)
        acts = [land(i, f, arrived) for f in range(FRAMES_HERE)]
        send(i)
        for f in range(FRAMES_HERE):
            spread(i, f, acts[f])
        own_taps(i)

    @pl.when(paired)
    def _():
        halo_taps()

    wait_all(packed.at[last], recv.at[last], send_sem.at[last], recv_sem.at[last])
    arrived = gathered(last)
    acts = {}
    for f in (1, 0):
        acts[f] = land(last, f, arrived)
        send(last + 1 - f)
    for f in (1, 0):
        spread(last, f, acts[f])
    own_taps(last)

    @pl.when(jnp.logical_not(paired))
    def _():
        halo_taps()

    loads[2].wait()
    time_bias = time_bias_ref[...][None, :]

    def mix(value, j):
        return jnp.dot(value, time_w[j], preferred_element_type=f32)

    receive(last)
    store_shifted(halo_windows.at[last, 1], H, act_halo[last, 1].astype(f32))
    resid_own[1] = (acc[1] + keep[1][0] * taps(last, 0, late, halo_windows)).astype(bf16)
    send(resid)
    acc[0] += keep[0][1] * taps(last, 1, late, halo_windows)
    receive(last + 1)
    store_shifted(halo_windows.at[last, 0], H, act_halo[last, 0].astype(f32))
    resid_own[0] = (acc[0] + keep[0][0] * taps(last, 0, early, halo_windows)).astype(bf16)
    send(resid + 1)
    temporal[1] = mix(resid_own[1], 2) + time_bias
    temporal[1] += keep[1][1] * mix(resid_own[0], 1)
    temporal[0] = mix(resid_own[0], 2) + time_bias

    bias = bias_row[...]
    bias = (bias + pltpu.roll(bias, up_channels, 1))[0:1]
    edge = jnp.zeros((H, 128), f32)
    lane_index = lax.broadcasted_iota(jnp.int32, (PIXELS, 128), 1)

    def enlarge(f):
        for half in range(2):
            frame = temporal[f, :, half * channels : (half + 1) * channels]
            store_shifted(enlarged.at[2 * f + half], 0, frame.astype(bf16).astype(f32))

    def upscale(f):
        for p in range(2):
            lhs = enlarged[2 * f : 2 * f + 2, :, p * channels : (p + 2) * channels]
            product = jnp.dot(
                lhs.reshape(2 * PIXELS, 2 * channels), up_w[p], preferred_element_type=f32
            )
            for half in range(2):
                rows = slice(half * PIXELS, (half + 1) * PIXELS)
                for t in range(pair // 128):
                    same = product[rows, t * 128 : (t + 1) * 128]
                    side = product[rows, pair + t * 128 : pair + (t + 1) * 128]
                    before_it = jnp.concatenate([edge, side[: PIXELS - H]], 0)
                    after_it = jnp.concatenate([side[H:], edge], 0)
                    if (t + 1) * 128 <= up_channels:
                        moved = before_it
                    elif t * 128 >= up_channels:
                        moved = after_it
                    else:
                        moved = jnp.where(lane_index < up_channels - t * 128, before_it, after_it)
                    woven[half, t, pl.ds(p, PIXELS, stride=2), :] = (
                        same + moved + bias[:, t * 128 : (t + 1) * 128]
                    )
        for half in range(2):
            for t in range(pair // 128):
                value = woven[half, t].astype(bf16)
                for x in range(W):
                    base = x * pair + t * 128
                    out_ref[2 * f + half, :, base : base + 128] = value[
                        x * 2 * H : (x + 1) * 2 * H
                    ]

    receive(resid)
    temporal[1] += keep[1][0] * mix(resid_halo[1], 0)
    enlarge(1)
    upscale(1)
    temporal[0] += keep[0][1] * mix(resid_halo[1], 1)
    receive(resid + 1)
    temporal[0] += keep[0][0] * mix(resid_halo[0], 0)
    enlarge(0)
    upscale(0)

    for i in range(len(hops)):
        sent(i)


def on_device(
    latent,
    owner,
    frame_counts,
    norm_gain,
    norm_shift,
    res_kernel,
    res_bias,
    time_kernel,
    time_bias,
    up_kernel,
    up_bias,
):
    n = lax.axis_size("tm")
    tokens, channels = latent.shape
    capacity = 2 * tokens // n
    up_channels = up_kernel.shape[-1]
    cut = 128
    chunks = channels // cut
    f32, bf16 = jnp.float32, jnp.bfloat16
    vmem = pl.BlockSpec(memory_space=pltpu.VMEM)
    smem = pl.BlockSpec(memory_space=pltpu.SMEM)
    hbm = pl.BlockSpec(memory_space=pl.ANY)
    frame = (FRAMES_HERE, PIXELS)
    return pl.pallas_call(
        functools.partial(kernel, n),
        out_shape=pltpu.VMEM((2 * FRAMES_HERE, 2 * H, 2 * W * up_channels), bf16),
        in_specs=[vmem, smem, vmem, vmem, vmem, vmem, vmem, vmem, hbm, hbm, hbm],
        out_specs=vmem,
        scratch_shapes=[
            pltpu.VMEM(res_kernel.shape, bf16),
            pltpu.VMEM(time_kernel.shape, bf16),
            pltpu.VMEM((3, 3, up_channels, channels), bf16),
            pltpu.VMEM((2, 2 * channels, 4 * up_channels), bf16),
            pltpu.VMEM((chunks, n, capacity, cut), bf16),
            pltpu.VMEM((chunks, n, capacity, cut), bf16),
            pltpu.VMEM((*frame, n * capacity), bf16),
            pltpu.VMEM((n, 1, 128), f32),
            pltpu.VMEM((n, 1, 128), f32),
            pltpu.VMEM((*frame, channels), f32),
            pltpu.VMEM((chunks, *frame, cut), bf16),
            pltpu.VMEM((chunks, *frame, cut), bf16),
            pltpu.VMEM((*frame, channels), bf16),
            pltpu.VMEM((*frame, channels), bf16),
            pltpu.VMEM((chunks, FRAMES_HERE, PIXELS + 2 * H, 3 * cut), bf16),
            pltpu.VMEM((chunks, FRAMES_HERE, PIXELS + 2 * H, 3 * cut), bf16),
            pltpu.VMEM((*frame, 2 * channels), f32),
            pltpu.VMEM((2 * FRAMES_HERE, PIXELS, 3 * channels), bf16),
            pltpu.VMEM((2, 2 * up_channels // 128, 2 * PIXELS, 128), f32),
            pltpu.VMEM((4 * up_channels, channels), f32),
            pltpu.VMEM((8, 2 * up_channels), f32),
            pltpu.SemaphoreType.DMA((3,)),
            pltpu.SemaphoreType.DMA((chunks,)),
            pltpu.SemaphoreType.DMA((chunks,)),
            pltpu.SemaphoreType.DMA,
            pltpu.SemaphoreType.DMA,
            pltpu.SemaphoreType.DMA((chunks + 3,)),
            pltpu.SemaphoreType.DMA((chunks + 3,)),
            pltpu.SemaphoreType.REGULAR((max(n.bit_length() - 2, 1),)),
        ],
        compiler_params=pltpu.CompilerParams(
            collective_id=0, has_side_effects=True, vmem_limit_bytes=60 << 20
        ),
    )(
        owner.reshape(1, tokens),
        frame_counts,
        latent,
        norm_gain,
        norm_shift,
        res_bias,
        time_bias,
        up_bias,
        res_kernel,
        time_kernel,
        up_kernel.swapaxes(2, 3),
    )


def solution(mesh):
    placed = (
        P(("groups", "tm"), None),
        P(("groups", "tm")),
        P("groups"),
        P(),
        P(),
        P(),
        P(),
        P(),
        P(),
        P(),
        P(),
    )
    return jax.shard_map(
        on_device,
        mesh=mesh,
        in_specs=placed,
        out_specs=P(("groups", "tm"), None, None),
        check_vma=False,
    )
```

```python
import functools
import math

import jax
import jax.numpy as jnp
from jax import lax
from jax.experimental import pallas as pl
from jax.experimental.pallas import tpu as pltpu
from jax.sharding import PartitionSpec as P

H = 16
W = 16
PIXELS = H * W
FRAMES_HERE = 2
MESH = pl.DeviceIdType.MESH

epsilon = 1e-06


def kernel(
    n,
    owner_ref,
    counts_ref,
    latent_ref,
    gain_ref,
    shift_ref,
    res_bias_ref,
    time_bias_ref,
    up_bias_ref,
    res_hbm,
    time_hbm,
    up_hbm,
    out_ref,
    res_w,
    time_w,
    up_raw,
    up_w,
    packed,
    recv,
    order,
    meta_out,
    meta_in,
    acc,
    act_own,
    act_halo,
    resid_own,
    resid_halo,
    windows,
    halo_windows,
    temporal,
    enlarged,
    woven,
    stack_w,
    bias_row,
    load_sem,
    send_sem,
    recv_sem,
    meta_send_sem,
    meta_recv_sem,
    halo_send_sem,
    halo_recv_sem,
    known_sem,
):
    me = lax.axis_index("tm")
    tokens, channels = latent_ref.shape
    chunks, _, capacity, cut = packed.shape
    slots = n * capacity
    up_channels = up_raw.shape[2]
    pair = 2 * up_channels
    f32, bf16 = jnp.float32, jnp.bfloat16

    barrier = pltpu.get_barrier_semaphore()

    bits = [1 << b for b in range(n.bit_length() - 1)]
    assert n == 1 << len(bits)

    def partner(k):
        return me + sum(b * (1 - 2 * lax.rem(me // b, 2)) for b in bits if k & b)

    def greet(semaphore, k):
        pl.semaphore_signal(
            semaphore, inc=1, device_id={"tm": partner(k)}, device_id_type=MESH
        )

    for b in bits:
        greet(barrier, b)

    loads = [
        pltpu.make_async_copy(src, dst, load_sem.at[i])
        for i, (src, dst) in enumerate(((up_hbm, up_raw), (res_hbm, res_w), (time_hbm, time_w)))
    ]
    for load in loads:
        load.start()

    owner = owner_ref[...]
    relative = lax.rem(owner - me + n, n)
    peers = lax.broadcasted_iota(jnp.int32, (n, tokens), 0)
    marked = (relative == peers).astype(f32)
    earlier = (
        lax.broadcasted_iota(jnp.int32, (tokens, tokens), 0)
        < lax.broadcasted_iota(jnp.int32, (tokens, tokens), 1)
    ).astype(f32).astype(bf16)
    before = jnp.dot(marked.astype(bf16), earlier, preferred_element_type=f32)
    rank = jnp.sum(before * marked, 0, keepdims=True).astype(jnp.int32)
    position = relative * capacity + rank

    per_group = 128 // capacity
    squares = latent_ref[...].astype(f32)
    squares = jnp.mean(squares * squares, -1, keepdims=True)
    scales = jnp.broadcast_to(lax.rsqrt(squares + epsilon), (tokens, 128)).T[0:1]
    lane = lax.rem(me, per_group) * capacity + rank
    lanes = lax.broadcasted_iota(jnp.int32, (128, tokens), 0)
    in_lane = (lanes == lane).astype(f32).astype(bf16)
    rest, scale_rows = scales, None
    for _ in range(3):
        piece = rest.astype(bf16).astype(f32)
        rest = rest - piece
        term = lax.dot_general(
            (marked * piece).astype(bf16),
            in_lane,
            (((1,), (1,)), ((), ())),
            preferred_element_type=f32,
        )
        scale_rows = term if scale_rows is None else scale_rows + term
    meta_out[...] = scale_rows[:, None, :]
    part = min(slots, 256)
    for c in range(slots // part):
        rows = lax.broadcasted_iota(jnp.int32, (part, tokens), 0) + c * part
        chosen = (rows == position).astype(f32).astype(bf16)
        block = jnp.dot(chosen, latent_ref[...], preferred_element_type=f32)
        per = part // capacity
        for i in range(chunks):
            packed[i, c * per : (c + 1) * per] = (
                block[:, i * cut : (i + 1) * cut].reshape(per, capacity, cut).astype(bf16)
            )

    pl.semaphore_wait(barrier, len(bits))

    def post(i, peer):
        pltpu.make_async_remote_copy(
            src_ref=packed.at[i, lax.rem(peer - me + n, n)],
            dst_ref=recv.at[i, me],
            send_sem=send_sem.at[i],
            recv_sem=recv_sem.at[i],
            device_id={"tm": peer},
            device_id_type=MESH,
        ).start()

    def open_with(offsets):
        for k in sorted(offsets, reverse=True):
            peer = partner(k)
            pltpu.make_async_remote_copy(
                src_ref=meta_out.at[lax.rem(peer - me + n, n)],
                dst_ref=meta_in.at[me],
                send_sem=meta_send_sem,
                recv_sem=meta_recv_sem,
                device_id={"tm": peer},
                device_id_type=MESH,
            ).start()
            post(0, peer)

    known = set(bits)
    for r, b in enumerate(bits[:-1]):
        greet(known_sem.at[r], b)
        open_with(known if r == 0 else known - older)
        older = set(known)
        known |= {b ^ k for k in known if k != b}
        pl.semaphore_wait(known_sem.at[r], 1)
    open_with(known - older)

    for i in range(1, chunks):

        @pl.loop(1, n)
        def _(k):
            post(i, lax.rem(me + k, n))

    meta_in[me] = meta_out[0]
    for i in range(chunks):
        recv[i, me] = packed[i, 0]

    border = jnp.zeros((H, 3 * cut), bf16)
    for i in range(chunks):
        for f in range(FRAMES_HERE):
            windows[i, f, 0:H] = border
            windows[i, f, H + PIXELS : 2 * H + PIXELS] = border
            halo_windows[i, f, 0:H] = border
            halo_windows[i, f, H + PIXELS : 2 * H + PIXELS] = border

    @pl.when(me == 0)
    def _():
        act_halo[...] = jnp.zeros_like(act_halo)
        resid_halo[...] = jnp.zeros_like(resid_halo)

    bias_row[...] = jnp.zeros_like(bias_row)
    bias_row[0:1, 0:up_channels] = up_bias_ref[...][None, :]
    loads[0].wait()
    folds = (((0,), (1, 2)), ((0, 1), (2,)))
    columns = ((1, 2), (0, 1), (0,), (2,))
    for p in range(2):
        for i in range(2):
            for r, taps in enumerate(columns):
                total = None
                for a in folds[p][i]:
                    for b in taps:
                        term = up_raw[a, b].astype(f32)
                        total = term if total is None else total + term
                stack_w[r * up_channels : (r + 1) * up_channels] = total
            for t in range(2 * pair // 128):
                up_w[p, i * channels : (i + 1) * channels, t * 128 : (t + 1) * 128] = (
                    stack_w[t * 128 : (t + 1) * 128].T.astype(bf16)
                )

    first = me * FRAMES_HERE
    keep = []
    for f in range(FRAMES_HERE):
        start = jnp.int32(0)
        begin = jnp.int32(0)
        for v in range(counts_ref.shape[0]):
            start = jnp.where(begin <= first + f, begin, start)
            begin = begin + counts_ref[v]
        keep.append(
            [jnp.where(first + f - 2 + j >= start, 1.0, 0.0).astype(f32) for j in range(2)]
        )

    def wait_all(src, dst, s_sem, r_sem):
        both = pltpu.make_async_remote_copy(
            src_ref=src.at[pl.ds(0, n - 1)],
            dst_ref=dst.at[pl.ds(0, n - 1)],
            send_sem=s_sem,
            recv_sem=r_sem,
            device_id={"tm": lax.rem(me + 1, n)},
            device_id_type=MESH,
        )
        both.wait_recv()
        both.wait_send()

    wait_all(meta_out, meta_in, meta_send_sem, meta_recv_sem)
    given = jnp.sum(jnp.where(meta_in[:, 0, :] > 0.0, 1.0, 0.0), 1, keepdims=True)
    slot = lax.broadcasted_iota(jnp.int32, (n, slots), 1)
    source = lax.broadcasted_iota(jnp.int32, (n, slots), 0)
    of_slot = slot // capacity
    here = jnp.sum(jnp.where(of_slot == source, given, 0.0), 0, keepdims=True).astype(jnp.int32)
    ahead = jnp.sum(jnp.where(source < of_slot, given, 0.0), 0, keepdims=True).astype(jnp.int32)
    row = lax.rem(slot[0:1], capacity)
    place = ahead + row
    pixel = lax.rem(place, PIXELS)
    place = place - pixel + lax.rem(pixel, W) * H + pixel // W
    place = jnp.where(row < here, place, -1)

    scale_of = jnp.concatenate(
        [
            jnp.sum(meta_in[g * per_group : (g + 1) * per_group, 0, :], 0, keepdims=True)
            for g in range(slots // 128)
        ],
        1,
    )
    row_scale = []
    for f in range(FRAMES_HERE):
        rows = lax.broadcasted_iota(jnp.int32, (PIXELS, slots), 0) + f * PIXELS
        chosen = rows == place
        order[f] = chosen.astype(f32).astype(bf16)
        row_scale.append(jnp.sum(jnp.where(chosen, scale_of, 0.0), 1, keepdims=True))
        acc[f] = jnp.broadcast_to(res_bias_ref[...][None, :], (PIXELS, channels))

    gain, shift = gain_ref[...][None, :], shift_ref[...][None, :]

    def store_shifted(target, top, value):
        width = value.shape[1]
        y_index = lax.rem(lax.broadcasted_iota(jnp.int32, value.shape, 0), H)
        above = jnp.where(y_index == 0, 0.0, pltpu.roll(value, 1, 0))
        below = jnp.where(y_index == H - 1, 0.0, pltpu.roll(value, PIXELS - 1, 0))
        for a, piece in enumerate((above, value, below)):
            target[top : top + PIXELS, a * width : (a + 1) * width] = piece.astype(bf16)

    right = lax.rem(me + 1, n)

    def hop(i, own, halo):
        return pltpu.make_async_remote_copy(
            src_ref=own,
            dst_ref=halo,
            send_sem=halo_send_sem.at[i],
            recv_sem=halo_recv_sem.at[i],
            device_id={"tm": right},
            device_id_type=MESH,
        )

    hops = [(act_own.at[i], act_halo.at[i]) for i in range(chunks - 1)]
    for owned, halo in ((act_own.at[chunks - 1], act_halo.at[chunks - 1]), (resid_own, resid_halo)):
        hops += [(owned.at[1], halo.at[1]), (owned.at[0], halo.at[0])]
    last = chunks - 1
    resid = chunks + 1

    def send(i):
        @pl.when(me < n - 1)
        def _():
            hop(i, *hops[i]).start()

    def receive(i):
        @pl.when(me > 0)
        def _():
            hop(i, *hops[i]).wait_recv()

    def sent(i):
        @pl.when(me < n - 1)
        def _():
            hop(i, *hops[i]).wait_send()

    def gathered(i):
        if capacity % 16:
            return recv[i].astype(f32).reshape(slots, cut).astype(bf16)
        return recv[i].reshape(slots, cut)

    def land(i, f, arrived):
        lo, hi = i * cut, (i + 1) * cut
        values = jnp.dot(order[f], arrived, preferred_element_type=f32)
        u = values * row_scale[f] * gain[:, lo:hi] + shift[:, lo:hi]
        act = (u / (1.0 + jnp.exp(-u))).astype(bf16)
        acc[f, :, lo:hi] += values
        act_own[i, f] = act
        return act.astype(f32)

    def spread(i, f, act):
        store_shifted(windows.at[i, f], H, act)

    def taps(i, j, frames, source=windows):
        lo, hi = i * cut, (i + 1) * cut
        weights = jnp.concatenate([res_w[j, a, b, lo:hi] for b in range(3) for a in range(3)], 0)
        lhs = jnp.concatenate(
            [
                source[i, frames, b * H : b * H + PIXELS, :].reshape(-1, 3 * cut)
                for b in range(3)
            ],
            1,
        )
        return jnp.dot(lhs, weights, preferred_element_type=f32)

    both, early, late = slice(0, FRAMES_HERE), slice(0, 1), slice(1, 2)

    def own_taps(i):
        acc[...] += taps(i, 2, both).reshape(FRAMES_HERE, PIXELS, channels)
        acc[1] += keep[1][1] * taps(i, 1, early)

    def halo_taps():
        for i in range(chunks - 1):
            receive(i)
            for f in range(FRAMES_HERE):
                store_shifted(halo_windows.at[i, f], H, act_halo[i, f].astype(f32))
            oldest = taps(i, 0, both, halo_windows)
            acc[0] += keep[0][0] * oldest[:PIXELS]
            acc[1] += keep[1][0] * oldest[PIXELS:]
            acc[0] += keep[0][1] * taps(i, 1, late, halo_windows)

    paired = lax.rem(me, 2) == 1
    loads[1].wait()
    for i in range(chunks - 1):
        wait_all(packed.at[i], recv.at[i], send_sem.at[i], recv_sem.at[i])
        arrived = gathered(i)
        acts = [land(i, f, arrived) for f in range(FRAMES_HERE)]
        send(i)
        for f in range(FRAMES_HERE):
            spread(i, f, acts[f])
        own_taps(i)

    @pl.when(paired)
    def _():
        halo_taps()

    wait_all(packed.at[last], recv.at[last], send_sem.at[last], recv_sem.at[last])
    arrived = gathered(last)
    acts = {}
    for f in (1, 0):
        acts[f] = land(last, f, arrived)
        send(last + 1 - f)
    for f in (1, 0):
        spread(last, f, acts[f])
    acc[1] += taps(last, 2, late)
    acc[1] += keep[1][1] * taps(last, 1, early)

    @pl.when(jnp.logical_not(paired))
    def _():
        halo_taps()

    loads[2].wait()
    time_bias = time_bias_ref[...][None, :]

    def mix(value, j):
        return jnp.dot(value, time_w[j], preferred_element_type=f32)

    receive(last)
    store_shifted(halo_windows.at[last, 1], H, act_halo[last, 1].astype(f32))
    resid_own[1] = (acc[1] + keep[1][0] * taps(last, 0, late, halo_windows)).astype(bf16)
    send(resid)
    acc[0] += taps(last, 2, early)
    acc[0] += keep[0][1] * taps(last, 1, late, halo_windows)
    receive(last + 1)
    store_shifted(halo_windows.at[last, 0], H, act_halo[last, 0].astype(f32))
    resid_own[0] = (acc[0] + keep[0][0] * taps(last, 0, early, halo_windows)).astype(bf16)
    send(resid + 1)
    temporal[1] = mix(resid_own[1], 2) + time_bias
    temporal[1] += keep[1][1] * mix(resid_own[0], 1)
    temporal[0] = mix(resid_own[0], 2) + time_bias

    bias = bias_row[...]
    bias = (bias + pltpu.roll(bias, up_channels, 1))[0:1]
    edge = jnp.zeros((H, 128), f32)
    lane_index = lax.broadcasted_iota(jnp.int32, (PIXELS, 128), 1)

    def enlarge(f):
        for half in range(2):
            frame = temporal[f, :, half * channels : (half + 1) * channels]
            store_shifted(enlarged.at[2 * f + half], 0, frame.astype(bf16).astype(f32))

    def upscale(f):
        for p in range(2):
            lhs = enlarged[2 * f : 2 * f + 2, :, p * channels : (p + 2) * channels]
            product = jnp.dot(
                lhs.reshape(2 * PIXELS, 2 * channels), up_w[p], preferred_element_type=f32
            )
            for half in range(2):
                rows = slice(half * PIXELS, (half + 1) * PIXELS)
                for t in range(pair // 128):
                    same = product[rows, t * 128 : (t + 1) * 128]
                    side = product[rows, pair + t * 128 : pair + (t + 1) * 128]
                    before_it = jnp.concatenate([edge, side[: PIXELS - H]], 0)
                    after_it = jnp.concatenate([side[H:], edge], 0)
                    if (t + 1) * 128 <= up_channels:
                        moved = before_it
                    elif t * 128 >= up_channels:
                        moved = after_it
                    else:
                        moved = jnp.where(lane_index < up_channels - t * 128, before_it, after_it)
                    woven[half, t, pl.ds(p, PIXELS, stride=2), :] = (
                        same + moved + bias[:, t * 128 : (t + 1) * 128]
                    )
        for half in range(2):
            for t in range(pair // 128):
                value = woven[half, t].astype(bf16)
                for x in range(W):
                    base = x * pair + t * 128
                    out_ref[2 * f + half, :, base : base + 128] = value[
                        x * 2 * H : (x + 1) * 2 * H
                    ]

    receive(resid)
    temporal[1] += keep[1][0] * mix(resid_halo[1], 0)
    enlarge(1)
    upscale(1)
    temporal[0] += keep[0][1] * mix(resid_halo[1], 1)
    receive(resid + 1)
    temporal[0] += keep[0][0] * mix(resid_halo[0], 0)
    enlarge(0)
    upscale(0)

    for i in range(len(hops)):
        sent(i)


def on_device(
    latent,
    owner,
    frame_counts,
    norm_gain,
    norm_shift,
    res_kernel,
    res_bias,
    time_kernel,
    time_bias,
    up_kernel,
    up_bias,
):
    n = lax.axis_size("tm")
    tokens, channels = latent.shape
    capacity = 2 * tokens // n
    up_channels = up_kernel.shape[-1]
    cut = 128
    chunks = channels // cut
    f32, bf16 = jnp.float32, jnp.bfloat16
    vmem = pl.BlockSpec(memory_space=pltpu.VMEM)
    smem = pl.BlockSpec(memory_space=pltpu.SMEM)
    hbm = pl.BlockSpec(memory_space=pl.ANY)
    frame = (FRAMES_HERE, PIXELS)
    return pl.pallas_call(
        functools.partial(kernel, n),
        out_shape=pltpu.VMEM((2 * FRAMES_HERE, 2 * H, 2 * W * up_channels), bf16),
        in_specs=[vmem, smem, vmem, vmem, vmem, vmem, vmem, vmem, hbm, hbm, hbm],
        out_specs=vmem,
        scratch_shapes=[
            pltpu.VMEM(res_kernel.shape, bf16),
            pltpu.VMEM(time_kernel.shape, bf16),
            pltpu.VMEM((3, 3, up_channels, channels), bf16),
            pltpu.VMEM((2, 2 * channels, 4 * up_channels), bf16),
            pltpu.VMEM((chunks, n, capacity, cut), bf16),
            pltpu.VMEM((chunks, n, capacity, cut), bf16),
            pltpu.VMEM((*frame, n * capacity), bf16),
            pltpu.VMEM((n, 1, 128), f32),
            pltpu.VMEM((n, 1, 128), f32),
            pltpu.VMEM((*frame, channels), f32),
            pltpu.VMEM((chunks, *frame, cut), bf16),
            pltpu.VMEM((chunks, *frame, cut), bf16),
            pltpu.VMEM((*frame, channels), bf16),
            pltpu.VMEM((*frame, channels), bf16),
            pltpu.VMEM((chunks, FRAMES_HERE, PIXELS + 2 * H, 3 * cut), bf16),
            pltpu.VMEM((chunks, FRAMES_HERE, PIXELS + 2 * H, 3 * cut), bf16),
            pltpu.VMEM((*frame, 2 * channels), f32),
            pltpu.VMEM((2 * FRAMES_HERE, PIXELS, 3 * channels), bf16),
            pltpu.VMEM((2, 2 * up_channels // 128, 2 * PIXELS, 128), f32),
            pltpu.VMEM((4 * up_channels, channels), f32),
            pltpu.VMEM((8, 2 * up_channels), f32),
            pltpu.SemaphoreType.DMA((3,)),
            pltpu.SemaphoreType.DMA((chunks,)),
            pltpu.SemaphoreType.DMA((chunks,)),
            pltpu.SemaphoreType.DMA,
            pltpu.SemaphoreType.DMA,
            pltpu.SemaphoreType.DMA((chunks + 3,)),
            pltpu.SemaphoreType.DMA((chunks + 3,)),
            pltpu.SemaphoreType.REGULAR((max(n.bit_length() - 2, 1),)),
        ],
        compiler_params=pltpu.CompilerParams(
            collective_id=0, has_side_effects=True, vmem_limit_bytes=60 << 20
        ),
    )(
        owner.reshape(1, tokens),
        frame_counts,
        latent,
        norm_gain,
        norm_shift,
        res_bias,
        time_bias,
        up_bias,
        res_kernel,
        time_kernel,
        up_kernel.swapaxes(2, 3),
    )


def solution(mesh):
    placed = (
        P(("groups", "tm"), None),
        P(("groups", "tm")),
        P("groups"),
        P(),
        P(),
        P(),
        P(),
        P(),
        P(),
        P(),
        P(),
    )
    return jax.shard_map(
        on_device,
        mesh=mesh,
        in_specs=placed,
        out_specs=P(("groups", "tm"), None, None),
        check_vma=False,
    )
```
